128 devices in a mesh: dp: 2 (over x_lo), width: 8 (over y, core), hidden: 8 (over z, x_hi).
Axes of the slice: x: 4 (x_hi: 2, x_lo: 2; x = x_hi * 2 + x_lo), y: 4, z: 4, core: 2. Of those that a mesh axis runs over, the one named last changes fastest.
Arguments:
- tokens: bfloat16 [1024, 8192], P('dp', 'width'), may hold values from -6 to 6
- target: bfloat16 [1024, 8192], P('dp', 'width'), may hold values from -6 to 6
- gate_weight: bfloat16 [8192, 14336], P('width', 'hidden'), may hold values from -0.0625 to 0.0625
- up_weight: bfloat16 [8192, 14336], P('width', 'hidden'), may hold values from -0.0625 to 0.0625
- down_weight: bfloat16 [14336, 8192], P('hidden', 'width'), may hold values from -0.046875 to 0.046875
- probe_sign: bfloat16 [8192, 14336], P('width', 'hidden'), may hold values from -1 to 1, as said below
Outputs:
- gate_grad: bfloat16 [8192, 14336], P(('width', 'dp'), 'hidden')
- hess_diag: bfloat16 [8192, 14336], P(('width', 'dp'), 'hidden')
The draws below stay inside these ranges and needn't reach their ends.
Inputs may be any that keep to these rules, and one draw needn't show every extreme that they name: `probe_sign`: every entry is -1 or +1.
All inputs are finite; a program needn't handle non-finite values.
Results may differ from the reference program's by a relative error of at most 0.019.
Values may be sent and summed in bfloat16 or wider, within the bound.
No kernel may reach another device: no remote copies, remote signals or barrier semaphores. Data moves between devices by JAX's collectives and lax.ppermute only.
A program may use at most 128 MiB of HBM per device.

```python
import math
import jax
import jax.numpy as jnp

D = 8192
FF = 14336
TOK_DEV = 512
TOKENS = 1024
N_DP = 2


def draw_probe_sign(key, part):
    coin_bits = jax.random.randint(key, (D, FF), 0, 2)
    return (2 * coin_bits - 1).astype(jnp.bfloat16)


def block_scale(rng, extent, shards, least, high):
    def one(axis_at, blocks):
        draws = jax.random.uniform(jax.random.fold_in(jax.random.fold_in(rng, 6), axis_at), (blocks,), jnp.float32, least / len(shards), high / len(shards))
        return jnp.repeat(jnp.exp(draws), extent[axis_at] // blocks).reshape((-1,) + (1,) * (len(extent) - axis_at - 1))

    gain = one(*shards[0])
    for cut in shards[1:]:
        gain = gain * one(*cut)
    return gain


def gaussian(own_key, extent, deviation, reach, split=(), dtype=jnp.bfloat16):
    result = deviation * jax.random.normal(own_key, extent, jnp.float32)
    if split:
        result = result * block_scale(own_key, extent, split, -0.22, 0.18)
    return jnp.clip(result, -reach, reach).astype(dtype)


def setup_inputs(seed: int = 0) -> dict:
    keys = jax.random.split(jax.random.key(seed), 7)
    return {
        "tokens": gaussian(keys[0], (TOKENS, D), 1.0, 6.0, ((0, 2), (1, 8))),
        "target": gaussian(keys[1], (TOKENS, D), 1.0, 6.0, ((0, 2), (1, 8))),
        "gate_weight": gaussian(keys[2], (D, FF), D ** -0.5, 0.0625, ((0, 8), (1, 8))),
        "up_weight": gaussian(keys[3], (D, FF), D ** -0.5, 0.0625, ((0, 8), (1, 8))),
        "down_weight": gaussian(keys[4], (FF, D), FF ** -0.5, 0.046875, ((0, 8), (1, 8))),
        "probe_sign": draw_probe_sign(jax.random.fold_in(keys[6], 71), 0),
    }


def reference(tokens, target, gate_weight, up_weight, down_weight, probe_sign):
    inv_width = 1.0 / math.sqrt(D)
    token_scale = 1.0 / math.sqrt(TOKENS)
    gate_pre = jnp.dot(tokens, gate_weight, preferred_element_type=jnp.float32)
    up_pre = jnp.dot(tokens, up_weight, preferred_element_type=jnp.float32)
    tangent = jnp.dot(tokens, probe_sign, preferred_element_type=jnp.float32) * inv_width
    sigmoid_gate = jax.nn.sigmoid(gate_pre)
    first = sigmoid_gate * (1.0 + gate_pre * (1.0 - sigmoid_gate))
    second = sigmoid_gate * (1.0 - sigmoid_gate) * (2.0 + gate_pre * (1.0 - 2.0 * sigmoid_gate))
    hidden = (gate_pre * sigmoid_gate * up_pre).astype(jnp.bfloat16)
    hidden_dot = (first * tangent * up_pre).astype(jnp.bfloat16)
    coeff_first = (first * up_pre).astype(jnp.bfloat16)
    coeff_second = (second * tangent * up_pre).astype(jnp.bfloat16)
    output = jnp.dot(hidden, down_weight, preferred_element_type=jnp.float32)
    output_dot = jnp.dot(hidden_dot, down_weight, preferred_element_type=jnp.float32)
    resid = (output - target.astype(jnp.float32)).astype(jnp.bfloat16)
    output_dot_b = output_dot.astype(jnp.bfloat16)
    back = jnp.dot(resid, down_weight.T, preferred_element_type=jnp.float32)
    back_dot = jnp.dot(output_dot_b, down_weight.T, preferred_element_type=jnp.float32)
    err_grad = (back * coeff_first.astype(jnp.float32)).astype(jnp.bfloat16)
    err_hess = (back * coeff_second.astype(jnp.float32) + back_dot * coeff_first.astype(jnp.float32)).astype(jnp.bfloat16)
    grad_sum = jnp.zeros((D, FF), jnp.float32)
    hv_sum = jnp.zeros((D, FF), jnp.float32)
    for half in range(N_DP):
        lower = half * TOK_DEV
        tok_half = tokens[lower:lower + TOK_DEV]
        grad_part = jnp.dot(tok_half.T, err_grad[lower:lower + TOK_DEV], preferred_element_type=jnp.float32) * token_scale
        hv_part = jnp.dot(tok_half.T, err_hess[lower:lower + TOK_DEV], preferred_element_type=jnp.float32) * token_scale
        grad_sum = grad_sum + grad_part.astype(jnp.bfloat16).astype(jnp.float32)
        hv_sum = hv_sum + hv_part.astype(jnp.bfloat16).astype(jnp.float32)
    gate_grad = grad_sum.astype(jnp.bfloat16)
    hess_diag = (probe_sign.astype(jnp.float32) * hv_sum * inv_width).astype(jnp.bfloat16)
    return (gate_grad, hess_diag)
```

```python
import functools
import math

import jax
import jax.numpy as jnp
from jax import lax
from jax.experimental import pallas as pl
from jax.experimental.pallas import tpu as pltpu
from jax.sharding import Mesh, PartitionSpec as P

D = 8192
CHUNKS = 2
RING = True
TILE = 256
BF = jnp.bfloat16
F32 = jnp.float32
NY = 4
NZ = 4
VMEM_LIMIT = 56 * 1024 * 1024


def shift(value, axis, step):
    size = lax.axis_size(axis)
    return lax.ppermute(value, axis, [(i, (i + step) % size) for i in range(size)])


def shape(dims, dtype=BF):
    return jax.ShapeDtypeStruct(dims, dtype)


def nbytes(avals):
    return sum(math.prod(a.shape) * a.dtype.itemsize for a in avals)


def call(body, ids, args, in_specs, outs, out_specs, grid, scratch=(), flops=0):
    cost = pl.CostEstimate(
        flops=flops, bytes_accessed=nbytes(args) + nbytes(outs), transcendentals=0
    )
    return pl.pallas_call(
        body,
        out_shape=tuple(outs),
        grid_spec=pltpu.PrefetchScalarGridSpec(
            num_scalar_prefetch=1,
            grid=grid,
            in_specs=in_specs,
            out_specs=tuple(out_specs),
            scratch_shapes=list(scratch),
        ),
        compiler_params=pltpu.CompilerParams(vmem_limit_bytes=VMEM_LIMIT),
        cost_estimate=cost,
    )(ids, *args)


def whole(array):
    rank = len(array.shape)
    return pl.BlockSpec(array.shape, lambda *_: (0,) * rank)


def last_tiled(array, tile=TILE):
    rank = len(array.shape)
    return pl.BlockSpec(
        (*array.shape[:-1], tile), lambda j, ids: (0,) * (rank - 1) + (j,)
    )


def token_row(ids, chunk, core_rel, y_rel, rows):
    core = lax.rem(ids[2] + core_rel, 2)
    y = lax.rem(ids[1] + y_rel, NY)
    return pl.multiple_of((chunk * 8 + core * NY + y) * rows, rows)


def pre_products(ids, chunk, rows, tokens, weights):
    width, cols = weights[0].shape

    def body(ids, t_ref, *refs):
        w_refs, (own_ref, other_ref), lhs = refs[:3], refs[3:5], refs[5]

        @pl.when(pl.program_id(0) == 0)
        def _():
            for c in range(2):
                for y in range(NY):
                    at = (c * NY + y) * rows
                    lhs[at:at + rows, :] = t_ref[pl.ds(token_row(ids, chunk, c, y, rows), rows), :]

        for k, w_ref in enumerate(w_refs):
            acc = jnp.dot(lhs[...], w_ref[...], preferred_element_type=F32).astype(BF)
            acc = acc.reshape(2, NY, rows, TILE)
            own_ref[k] = acc[0]
            other_ref[k] = acc[1]

    out = shape((3, NY, rows, cols))
    return call(
        body, ids, (tokens, *weights),
        [whole(tokens)] + [last_tiled(w) for w in weights],
        [out, out], [last_tiled(out)] * 2, (cols // TILE,),
        [pltpu.VMEM((8 * rows, width), BF)],
        flops=3 * 2 * 8 * rows * width * cols,
    )


def split_sum(ids, own, recv, lead_axis):
    if lead_axis == 1:
        n, _, rows, cols = own.shape
        half = rows // 2
        low = lambda v: v[:, :half]
        high = lambda v: v[:, half:]
        pick = lambda ref, y: ref[:, y].astype(F32)
        full_dims, half_dims = (n, rows, cols), (n, half, cols)
    else:
        _, n, rows, cols = own.shape
        low = lambda v: v[0]
        high = lambda v: v[1]
        pick = lambda ref, y: ref[y].astype(F32)
        full_dims, half_dims = (n, rows, cols), (rows, cols)

    def body(ids, a_ref, b_ref, o0, o1l, o1h, o2l, o2h, o3l, o3h):
        total = [pick(a_ref, y) + pick(b_ref, y) for y in range(NY)]
        o0[...] = total[0]
        for y, (l_ref, h_ref) in ((1, (o1l, o1h)), (2, (o2l, o2h)), (3, (o3l, o3h))):
            l_ref[...] = low(total[y]).astype(BF)
            h_ref[...] = high(total[y]).astype(BF)

    outs = [shape(full_dims, F32)] + [shape(half_dims)] * 6
    return call(
        body, ids, (own, recv), [last_tiled(own)] * 2,
        outs, [last_tiled(o) for o in outs], (cols // TILE,),
    )


def add_pair(a, b):
    return (a.astype(F32) + b.astype(F32)).astype(BF)


def ring_scatter(blocks):
    own, b1l, b1h, b2l, b2h, b3l, b3h = blocks
    relay_low = shift(b2l, "y", 1)
    relay_high = shift(b2h, "y", -1)
    direct_high = shift(b1h, "y", 1)
    direct_low = shift(b3l, "y", -1)
    both_low = shift(add_pair(b1l, relay_low), "y", 1)
    both_high = shift(add_pair(b3h, relay_high), "y", -1)
    return own, (both_low, direct_low), (both_high, direct_high)


def coefficients(ids, own, lows, highs):
    n, rows, cols = own.shape
    half = rows // 2
    inv_width = 1.0 / math.sqrt(D)

    def body(ids, own_ref, l0, l1, h0, h1, pay_ref, first_ref, second_ref):
        for start, a, b in ((0, l0, l1), (half, h0, h1)):
            part = own_ref[:, start:start + half] + a[...].astype(F32) + b[...].astype(F32)
            gate, up, tangent = part[0], part[1], part[2] * inv_width
            sig = jax.nn.sigmoid(gate)
            first = sig * (1.0 + gate * (1.0 - sig)) * up
            second = sig * (1.0 - sig) * (2.0 + gate * (1.0 - 2.0 * sig)) * (tangent * up)
            pay_ref[0, start:start + half] = (gate * sig * up).astype(BF)
            pay_ref[1, start:start + half] = (first * tangent).astype(BF)
            first_ref[start:start + half] = first.astype(BF)
            second_ref[start:start + half] = second.astype(BF)

    outs = [shape((2, rows, cols)), shape((rows, cols)), shape((rows, cols))]
    args = (own, *lows, *highs)
    return call(
        body, ids, args, [last_tiled(a) for a in args],
        outs, [last_tiled(o) for o in outs], (cols // TILE,),
    )


def gather_y(value):
    return [value, shift(value, "y", -1), shift(value, "y", -2), shift(value, "y", -3)]


def gather_width(value):
    near = gather_y(value)
    return near + [shift(v, "core", 1) for v in near]


def down_products(ids, pieces, down):
    _, rows, cols = pieces[0].shape
    width = down.shape[1]
    tile = width // NZ
    total = 8 * 2 * rows

    def body(ids, *refs):
        p_refs, d_ref, o_refs, lhs = refs[:8], refs[8], refs[9:13], refs[13]
        j = pl.program_id(0)

        @pl.when(j == 0)
        def _():
            for i, p_ref in enumerate(p_refs):
                lhs[2 * rows * i:2 * rows * (i + 1), :] = p_ref[...].reshape(2 * rows, cols)

        acc = jnp.dot(lhs[...], d_ref[...], preferred_element_type=F32).astype(BF)
        for k, o_ref in enumerate(o_refs):
            @pl.when(j == k)
            def _(o_ref=o_ref):
                o_ref[...] = acc

    outs = [shape((total, tile))] * NZ
    return call(
        body, ids, (*pieces, down),
        [whole(p) for p in pieces]
        + [pl.BlockSpec((cols, tile), lambda j, ids: (0, lax.rem(ids[3] + j, NZ)))],
        outs, [whole(o) for o in outs], (NZ,),
        [pltpu.VMEM((total, cols), BF)],
        flops=2 * total * width * cols,
    )


def sum_z(ids, parts):
    rows, cols = parts[0].shape
    half = cols // 2

    def body(ids, a, b, c, d, own_ref, send_ref):
        total = a[...].astype(F32) + b[...].astype(F32) + c[...].astype(F32) + d[...].astype(F32)
        first = ids[4] == 0
        own_ref[...] = jnp.where(first, total[:, :half], total[:, half:])
        send_ref[...] = jnp.where(first, total[:, half:], total[:, :half]).astype(BF)

    outs = [shape((rows, half), F32), shape((rows, half))]
    return call(body, ids, parts, [whole(p) for p in parts], outs, [whole(o) for o in outs], (1,))


def residual(ids, chunk, rows, own, recv, target):
    total, cols = own.shape

    def body(ids, own_ref, recv_ref, t_ref, o_ref):
        column = pl.multiple_of((ids[3] * 2 + ids[4]) * cols, cols)
        for c in range(2):
            for y in range(NY):
                at = (c * NY + y) * 2 * rows
                value = own_ref[at:at + 2 * rows] + recv_ref[at:at + 2 * rows].astype(F32)
                goal = t_ref[pl.ds(token_row(ids, chunk, c, y, rows), rows), pl.ds(column, cols)]
                o_ref[at:at + rows] = (value[:rows] - goal.astype(F32)).astype(BF)
                o_ref[at + rows:at + 2 * rows] = value[rows:].astype(BF)

    out = shape((total, cols))
    args = (own, recv, target)
    return call(body, ids, args, [whole(a) for a in args], [out], [whole(out)], (1,))[0]


def join_pair(ids, own, recv):
    rows, cols = own.shape

    def body(ids, a, b, o_ref):
        first = ids[4] == 0
        o_ref[:, :cols] = jnp.where(first, a[...], b[...])
        o_ref[:, cols:] = jnp.where(first, b[...], a[...])

    out = shape((rows, 2 * cols))
    return call(body, ids, (own, recv), [whole(own)] * 2, [out], [whole(out)], (1,))[0]


def back_products(ids, parts, down, rows):
    total, tile_k = parts[0].shape
    cols, width = down.shape

    def body(ids, *refs):
        f_refs, d_ref, own_ref, other_ref = refs[:NZ], refs[NZ], refs[NZ + 1], refs[NZ + 2]
        acc = jnp.zeros((total, TILE), F32)
        for k, f_ref in enumerate(f_refs):
            at = pl.multiple_of(lax.rem(ids[3] + k, NZ) * tile_k, tile_k)
            acc += lax.dot_general(
                f_ref[...], d_ref[:, pl.ds(at, tile_k)], (((1,), (1,)), ((), ())),
                preferred_element_type=F32,
            )
        acc = acc.astype(BF).reshape(2, NY, 2, rows, TILE)
        own_ref[...] = acc[0]
        other_ref[...] = acc[1]

    out = shape((NY, 2, rows, cols))
    return call(
        body, ids, (*parts, down),
        [whole(p) for p in parts] + [pl.BlockSpec((TILE, width), lambda j, ids: (j, 0))],
        [out, out], [last_tiled(out)] * 2, (cols // TILE,),
        flops=2 * total * width * cols,
    )


def errors(ids, own, lows, highs, first, second):
    def body(ids, own_ref, l0, l1, h0, h1, f_ref, s_ref, o_ref):
        back = own_ref[0] + l0[...].astype(F32) + l1[...].astype(F32)
        back_dot = own_ref[1] + h0[...].astype(F32) + h1[...].astype(F32)
        f = f_ref[...].astype(F32)
        o_ref[0] = (back * f).astype(BF)
        o_ref[1] = (back * s_ref[...].astype(F32) + back_dot * f).astype(BF)

    out = shape(own.shape)
    args = (own, *lows, *highs, first, second)
    return call(
        body, ids, args, [last_tiled(a) for a in args],
        [out], [last_tiled(out)], (own.shape[-1] // TILE,),
    )[0]


def transposed_tokens(ids, tokens, other, rows):
    count, width = tokens.shape
    half = other.shape[1]
    chunks = count // (8 * rows)

    def body(ids, t_ref, x_ref, o_ref, held):
        at = 0
        for chunk in range(chunks):
            for ref in (t_ref, x_ref):
                for c in range(2):
                    for y in range(NY):
                        row = token_row(ids, chunk, c, y, rows)
                        held[at:at + rows, :] = ref[pl.ds(row, rows), :]
                        at += rows
        o_ref[...] = held[...].T

    out = shape((half, 2 * count))
    return call(
        body, ids, (tokens, other),
        [pl.BlockSpec((count, half), lambda j, ids: (0, ids[0])), whole(other)],
        [out], [whole(out)], (1,), [pltpu.VMEM((2 * count, half), BF)],
    )[0]


def outer_products(ids, lhs, pieces, probe):
    out_rows, count = lhs.shape
    _, rows, cols = pieces[0].shape
    token_scale = 1.0 / math.sqrt(count)
    inv_width = 1.0 / math.sqrt(D)
    n = len(pieces)

    def body(ids, l_ref, *refs):
        p_refs, probe_ref, g_ref, h_ref = refs[:n], refs[n], refs[n + 1], refs[n + 2]
        left = l_ref[...]
        err = jnp.concatenate([p[0] for p in p_refs], axis=0)
        g_ref[...] = (jnp.dot(left, err, preferred_element_type=F32) * token_scale).astype(BF)
        err = jnp.concatenate([p[1] for p in p_refs], axis=0)
        hv = jnp.dot(left, err, preferred_element_type=F32) * token_scale
        h_ref[...] = (probe_ref[...].astype(F32) * hv * inv_width).astype(BF)

    out = shape((out_rows, cols))
    return call(
        body, ids, (lhs, *pieces, probe),
        [whole(lhs)] + [last_tiled(p) for p in pieces]
        + [pl.BlockSpec((out_rows, TILE), lambda j, ids: (ids[0], j))],
        [out, out], [last_tiled(out)] * 2, (cols // TILE,),
        flops=4 * out_rows * count * cols,
    )


def on_device(tokens, target, gate_weight, up_weight, down_weight, probe_sign):
    ids = jnp.stack([lax.axis_index(a) for a in ("dp", "y", "core", "z", "xh")]).astype(jnp.int32)
    count, width = tokens.shape
    rows = count // (CHUNKS * 8)
    half = width // 2
    other_cols = lax.dynamic_slice_in_dim(tokens, (1 - ids[0]) * half, half, 1)
    other_tokens = shift(other_cols, "dp", 1)
    lhs = transposed_tokens(ids, tokens, other_tokens, rows)
    weights = (gate_weight, up_weight, probe_sign)
    pieces = []
    for chunk in range(CHUNKS):
        own, other = pre_products(ids, chunk, rows, tokens, weights)
        recv = shift(other, "core", 1)
        own, lows, highs = ring_scatter(split_sum(ids, own, recv, 1))
        pay, first, second = coefficients(ids, own, lows, highs)
        parts = down_products(ids, gather_width(pay), down_weight)
        parts = [parts[0]] + [shift(parts[k], "z", k) for k in range(1, NZ)]
        own, send = sum_z(ids, parts)
        err = residual(ids, chunk, rows, own, shift(send, "xh", 1), target)
        joined = join_pair(ids, err, shift(err, "xh", 1))
        parts = [joined] + [shift(joined, "z", -k) for k in range(1, NZ)]
        own, other = back_products(ids, parts, down_weight, rows)
        recv = shift(other, "core", 1)
        own, lows, highs = ring_scatter(split_sum(ids, own, recv, 0))
        err = errors(ids, own, lows, highs, first, second)
        far = shift(err, "dp", 1)
        pieces += gather_width(err) + gather_width(far)
    return outer_products(ids, lhs, pieces, probe_sign)


def solution(mesh):
    fine = Mesh(mesh.devices.reshape(2, 4, 2, 4, 2), ("dp", "y", "core", "z", "xh"))
    width, hidden = ("y", "core"), ("z", "xh")
    return jax.shard_map(
        on_device,
        mesh=fine,
        in_specs=(
            P("dp", width),
            P("dp", width),
            P(width, hidden),
            P(width, hidden),
            P(hidden, width),
            P(width, hidden),
        ),
        out_specs=(P(("y", "core", "dp"), hidden), P(("y", "core", "dp"), hidden)),
        check_vma=False,
    )
```

```python
import functools
import math

import jax
import jax.numpy as jnp
from jax import lax
from jax.experimental import pallas as pl
from jax.experimental.pallas import tpu as pltpu
from jax.sharding import Mesh, PartitionSpec as P

D = 8192
TILE = 256
BF = jnp.bfloat16
F32 = jnp.float32
NY = 4
NZ = 4
MIB = 1024 * 1024


def shift(value, axis, step):
    size = lax.axis_size(axis)
    return lax.ppermute(value, axis, [(i, (i + step) % size) for i in range(size)])


def shape(dims, dtype=BF):
    return jax.ShapeDtypeStruct(dims, dtype)


def nbytes(avals):
    return sum(math.prod(a.shape) * a.dtype.itemsize for a in avals)


def call(body, ids, args, outs, scratch=(), flops=0, limit=8, after=()):
    n = len(args)

    def kernel(ids, *refs):
        body(ids, *refs[:n], *refs[n + len(after):])

    cost = pl.CostEstimate(
        flops=flops, bytes_accessed=nbytes(args) + nbytes(outs), transcendentals=0
    )
    vmem = pl.BlockSpec(memory_space=pltpu.VMEM)
    return pl.pallas_call(
        kernel,
        out_shape=tuple(outs),
        in_specs=[pl.BlockSpec(memory_space=pltpu.SMEM)] + [vmem] * n + [pl.BlockSpec(memory_space=pl.ANY)] * len(after),
        out_specs=tuple([vmem] * len(outs)),
        scratch_shapes=list(scratch),
        compiler_params=pltpu.CompilerParams(vmem_limit_bytes=limit * MIB),
        cost_estimate=cost,
        name=body.__qualname__.split(".")[0],
    )(ids, *args, *after)


def loop_tiles(size, tile, body):
    def step(j, carry):
        body(pl.ds(pl.multiple_of(j * tile, tile), tile))
        return carry

    lax.fori_loop(0, size // tile, step, 0)


def token_row(ids, core_rel, y_rel, rows):
    core = lax.rem(ids[2] + core_rel, 2)
    y = lax.rem(ids[1] + y_rel, NY)
    return pl.multiple_of((core * NY + y) * rows, rows)


def ordered_tokens(ids, rows, tokens):
    width = tokens.shape[1]

    def body(ids, t_ref, o_ref):
        for c in range(2):
            for y in range(NY):
                at = (c * NY + y) * rows
                o_ref[at:at + rows, :] = t_ref[pl.ds(token_row(ids, c, y, rows), rows), :]

    return call(body, ids, (tokens,), [shape((8 * rows, width))])[0]


def pre_products(ids, rows, ordered, weight):
    width, cols = weight.shape

    def body(ids, t_ref, w_ref, own_ref, other_ref):
        def step(at):
            acc = jnp.dot(t_ref[...], w_ref[:, at], preferred_element_type=F32).astype(BF)
            acc = acc.reshape(2, NY, rows, TILE)
            own_ref[:, :, at] = acc[0]
            other_ref[:, :, at] = acc[1]

        loop_tiles(cols, TILE, step)

    out = shape((NY, rows, cols))
    return call(
        body, ids, (ordered, weight), [out, out], flops=2 * 8 * rows * width * cols
    )


def split_pre(ids, owns, recvs):
    n = len(owns)
    _, rows, cols = owns[0].shape
    half = rows // 2

    def body(ids, *refs):
        a_refs, b_refs = refs[:n], refs[n:2 * n]
        o0, o1l, o1h, o2l, o2h, o3l, o3h = refs[2 * n:]

        def step(at):
            for i in range(n):
                o0[i, :, at] = a_refs[i][0, :, at].astype(F32) + b_refs[i][0, :, at].astype(F32)
                for y, l_ref, h_ref in ((1, o1l, o1h), (2, o2l, o2h), (3, o3l, o3h)):
                    total = a_refs[i][y, :, at].astype(F32) + b_refs[i][y, :, at].astype(F32)
                    l_ref[i, :, at] = total[:half].astype(BF)
                    h_ref[i, :, at] = total[half:].astype(BF)

        loop_tiles(cols, TILE, step)

    outs = [shape((n, rows, cols), F32)] + [shape((n, half, cols))] * 6
    return call(body, ids, (*owns, *recvs), outs)


def add_pair(a, b):
    return (a.astype(F32) + b.astype(F32)).astype(BF)


def ring_scatter(blocks):
    own, b1l, b1h, b2l, b2h, b3l, b3h = blocks
    relay_low = shift(b2l, "y", 1)
    relay_high = shift(b2h, "y", -1)
    direct_high = shift(b1h, "y", 1)
    direct_low = shift(b3l, "y", -1)
    both_low = shift(add_pair(b1l, relay_low), "y", 1)
    both_high = shift(add_pair(b3h, relay_high), "y", -1)
    return own, (both_low, direct_low), (both_high, direct_high)


def coefficients(ids, own, lows, highs):
    n, rows, cols = own.shape
    half = rows // 2
    inv_width = 1.0 / math.sqrt(D)

    def body(ids, own_ref, l0, l1, h0, h1, low_ref, high_ref, first_ref, second_ref):
        def step(at):
            for start, a, b, pay_ref in ((0, l0, l1, low_ref), (half, h0, h1, high_ref)):
                to = slice(start, start + half)
                gate, up, tangent = (
                    own_ref[i, to, at] + a[i, :, at].astype(F32) + b[i, :, at].astype(F32)
                    for i in range(3)
                )
                tangent = tangent * inv_width
                sig = jax.nn.sigmoid(gate)
                first = sig * (1.0 + gate * (1.0 - sig)) * up
                second = sig * (1.0 - sig) * (2.0 + gate * (1.0 - 2.0 * sig)) * (tangent * up)
                pay_ref[0, :, at] = (gate * sig * up).astype(BF)
                pay_ref[1, :, at] = (first * tangent).astype(BF)
                first_ref[to, at] = first.astype(BF)
                second_ref[to, at] = second.astype(BF)

        loop_tiles(cols, TILE, step)

    pay = shape((2, half, cols))
    outs = [pay, pay, shape((rows, cols)), shape((rows, cols))]
    return call(body, ids, (own, *lows, *highs), outs)


def gather_y(value):
    return [value, shift(value, "y", -1), shift(value, "y", -2), shift(value, "y", -3)]


def swap_cores(values):
    return [shift(v, "core", 1) for v in values]


def ring_pair(near, far):
    near_low, near_high = shift(near, "y", 1), shift(near, "y", -1)
    far_low, far_high = shift(far, "y", 1), shift(far, "y", -1)
    across = shift(near_low, "y", 1), shift(far_high, "y", -1)
    return [near, far, near_high, far_high, *across, near_low, far_low]


def down_products(ids, pieces, down):
    _, rows, cols = pieces[0].shape
    width = down.shape[1]
    tile = width // NZ
    total = 8 * 2 * rows

    def body(ids, *refs):
        p_refs, d_ref, o_refs, lhs = refs[:8], refs[8], refs[9:13], refs[13]
        for i, p_ref in enumerate(p_refs):
            lhs[2 * rows * i:2 * rows * (i + 1), :] = p_ref[...].reshape(2 * rows, cols)

        def step(k, carry):
            at = pl.multiple_of(lax.rem(ids[3] + k, NZ) * tile, tile)
            acc = jnp.dot(
                lhs[...], d_ref[:, pl.ds(at, tile)], preferred_element_type=F32
            ).astype(BF)
            for i, o_ref in enumerate(o_refs):
                @pl.when(k == i)
                def _(o_ref=o_ref):
                    o_ref[...] = acc
            return carry

        lax.fori_loop(0, NZ, step, 0)

    outs = [shape((total, tile))] * NZ
    return call(
        body, ids, (*pieces, down), outs, [pltpu.VMEM((total, cols), BF)],
        flops=2 * total * width * cols, limit=12)


def spread(axis, blocks):
    first, *rest = blocks
    return [first] + [shift(v, axis, k + 1) for k, v in enumerate(rest)]


def sum_z(ids, parts):
    def body(ids, a, b, c, d, o_ref):
        total = a[...].astype(F32) + b[...].astype(F32) + c[...].astype(F32) + d[...].astype(F32)
        o_ref[...] = total.astype(BF)

    return call(body, ids, parts, [shape(parts[0].shape)])[0]


def residual(ids, chunk, rows, own, recv, target):
    total, cols = own.shape

    def body(ids, own_ref, recv_ref, t_ref, o_ref):
        column = pl.multiple_of(ids[3] * cols, cols)
        for c in range(2):
            for y in range(NY):
                at = (c * NY + y) * 2 * rows
                to = slice(at, at + 2 * rows)
                value = own_ref[to].astype(F32) + recv_ref[to].astype(F32)
                row = pl.multiple_of(token_row(ids, c, y, 2 * rows) + chunk * rows, rows)
                goal = t_ref[pl.ds(row, rows), pl.ds(column, cols)]
                o_ref[at:at + rows] = (value[:rows] - goal.astype(F32)).astype(BF)
                o_ref[at + rows:at + 2 * rows] = value[rows:].astype(BF)

    return call(body, ids, (own, recv, target), [shape((total, cols))])[0]


def back_products(ids, parts, down, rows, after=()):
    total, tile_k = parts[0].shape
    cols, width = down.shape

    def body(ids, *refs):
        f_refs, d_ref, own_ref, other_ref = refs[:NZ], refs[NZ], refs[NZ + 1], refs[NZ + 2]

        def step(at):
            acc = jnp.zeros((total, TILE), F32)
            for k, f_ref in enumerate(f_refs):
                to = pl.multiple_of(lax.rem(ids[3] + k, NZ) * tile_k, tile_k)
                acc += lax.dot_general(
                    f_ref[...], d_ref[at, pl.ds(to, tile_k)], (((1,), (1,)), ((), ())),
                    preferred_element_type=F32,
                )
            acc = acc.astype(BF).reshape(2, NY, 2, rows, TILE)
            own_ref[:, :, :, at] = acc[0]
            other_ref[:, :, :, at] = acc[1]

        loop_tiles(cols, TILE, step)

    out = shape((NY, 2, rows, cols))
    return call(
        body, ids, (*parts, down), [out, out], flops=2 * total * width * cols, limit=12, after=after)


def split_back(ids, own, recv):
    _, n, rows, cols = own.shape

    def body(ids, a_ref, b_ref, *outs):
        def step(at):
            for i in range(n):
                for y in range(NY):
                    total = a_ref[y, i, :, at].astype(F32) + b_ref[y, i, :, at].astype(F32)
                    outs[y][i, :, at] = total.astype(outs[y].dtype)

        loop_tiles(cols, TILE, step)

    outs = [shape((n, rows, cols), F32)] + [shape((n, rows, cols))] * 3
    return call(body, ids, (own, recv), outs)


def sum_at(refs, i, at):
    total = refs[0][i, :, at].astype(F32)
    for ref in refs[1:]:
        total += ref[i, :, at].astype(F32)
    return total


def errors(ids, chunk, terms, first, second, before=()):
    n, rows, cols = terms[0].shape

    def body(ids, *refs):
        (f_ref, s_ref), done, o_ref = refs[len(terms):len(terms) + 2], refs[len(terms) + 2:-1], refs[-1]
        mine = slice(chunk * rows, (chunk + 1) * rows)

        def step(at):
            back, back_dot = (sum_at(refs[:len(terms)], i, at) for i in range(2))
            f = f_ref[mine, at].astype(F32)
            o_ref[0, mine, at] = (back * f).astype(BF)
            o_ref[1, mine, at] = (back * s_ref[mine, at].astype(F32) + back_dot * f).astype(BF)
            for ref in done:
                o_ref[:, :chunk * rows, at] = ref[:, :, at]

        loop_tiles(cols, TILE, step)

    out = shape((n, (chunk + 1) * rows, cols))
    return call(body, ids, (*terms, first, second, *before), [out])[0]


def transposed_tokens(ids, tokens, other, rows):
    count, width = tokens.shape
    half = other.shape[1]

    def body(ids, t_ref, x_ref, o_ref, held):
        cols = pl.ds(pl.multiple_of(ids[0] * half, half), half)
        at = 0
        for c in range(2):
            for y in range(NY):
                row = pl.ds(token_row(ids, c, y, rows), rows)
                held[at:at + rows, :] = t_ref[row, cols]
                held[at + rows:at + 2 * rows, :] = x_ref[row, :]
                at += 2 * rows
        o_ref[...] = held[...].T

    return call(
        body, ids, (tokens, other), [shape((half, 2 * count))],
        [pltpu.VMEM((2 * count, half), BF)],
    )[0]


def outer_products(ids, lhs, pieces, probe):
    out_rows, count = lhs.shape
    _, rows, cols = pieces[0].shape
    token_scale = 1.0 / math.sqrt(count)
    inv_width = 1.0 / math.sqrt(D)
    n = len(pieces)

    def body(ids, l_ref, *refs):
        p_refs, probe_ref, g_ref, h_ref = refs[:n], refs[n], refs[n + 1], refs[n + 2]
        probe_rows = pl.ds(pl.multiple_of(ids[0] * out_rows, out_rows), out_rows)

        def step(at):
            err = jnp.concatenate([p[0, :, at] for p in p_refs], axis=0)
            g = jnp.dot(l_ref[...], err, preferred_element_type=F32) * token_scale
            g_ref[:, at] = g.astype(BF)
            err = jnp.concatenate([p[1, :, at] for p in p_refs], axis=0)
            hv = jnp.dot(l_ref[...], err, preferred_element_type=F32) * token_scale
            h_ref[:, at] = (probe_ref[probe_rows, at].astype(F32) * hv * inv_width).astype(BF)

        loop_tiles(cols, TILE, step)

    out = shape((out_rows, cols))
    return call(
        body, ids, (lhs, *pieces, probe), [out, out],
        flops=4 * out_rows * count * cols, limit=12,
    )


def on_device(tokens, target, gate_weight, up_weight, down_weight, probe_sign):
    ids = jnp.stack([lax.axis_index(a) for a in ("dp", "y", "core", "z", "xh")]).astype(jnp.int32)
    count, width = tokens.shape
    rows = count // 8
    half = width // 2
    other_cols = lax.dynamic_slice_in_dim(tokens, (1 - ids[0]) * half, half, 1)
    other_tokens = shift(other_cols, "dp", 1)
    lhs = transposed_tokens(ids, tokens, other_tokens, rows)
    ordered = ordered_tokens(ids, rows, tokens)
    pairs = [pre_products(ids, rows, ordered, w) for w in (gate_weight, up_weight, probe_sign)]
    recvs = swap_cores([other for _, other in pairs])
    own, lows, highs = ring_scatter(split_pre(ids, [own for own, _ in pairs], recvs))
    *pays, first, second = coefficients(ids, own, lows, highs)
    done = ()
    for c, pay in enumerate(pays):
        near = gather_y(pay)
        parts = spread("z", down_products(ids, near + swap_cores(near), down_weight))
        part = sum_z(ids, parts)
        err = residual(ids, c, rows // 2, part, shift(part, "xh", 1), target)
        parts = [err] + [shift(err, "z", -k) for k in range(1, NZ)]
        own, other = back_products(ids, parts, down_weight, rows // 2, () if c else (lhs,))
        terms = spread("y", split_back(ids, own, shift(other, "core", 1)))
        done = (errors(ids, c, terms, first, second, done),)
    near = ring_pair(done[0], shift(done[0], "dp", 1))
    return outer_products(ids, lhs, near + swap_cores(near), probe_sign)


def solution(mesh):
    fine = Mesh(mesh.devices.reshape(2, 4, 2, 4, 2), ("dp", "y", "core", "z", "xh"))
    width, hidden = ("y", "core"), ("z", "xh")
    return jax.shard_map(
        on_device,
        mesh=fine,
        in_specs=(
            P("dp", width),
            P("dp", width),
            P(width, hidden),
            P(width, hidden),
            P(hidden, width),
            P(width, hidden),
        ),
        out_specs=(P(("y", "core", "dp"), hidden), P(("y", "core", "dp"), hidden)),
        check_vma=False,
    )
```

```python
import functools
import math

import jax
import jax.numpy as jnp
from jax import lax
from jax.experimental import pallas as pl
from jax.experimental.pallas import tpu as pltpu
from jax.sharding import Mesh, PartitionSpec as P

D = 8192
TILE = 256
BF = jnp.bfloat16
F32 = jnp.float32
NY = 4
NZ = 4
MIB = 1024 * 1024


def shift(value, axis, step):
    size = lax.axis_size(axis)
    return lax.ppermute(value, axis, [(i, (i + step) % size) for i in range(size)])


def shape(dims, dtype=BF):
    return jax.ShapeDtypeStruct(dims, dtype)


def nbytes(avals):
    return sum(math.prod(a.shape) * a.dtype.itemsize for a in avals)


def call(body, ids, args, outs, scratch=(), flops=0, limit=8, after=()):
    n = len(args)

    def kernel(ids, *refs):
        body(ids, *refs[:n], *refs[n + len(after):])

    cost = pl.CostEstimate(
        flops=flops, bytes_accessed=nbytes(args) + nbytes(outs), transcendentals=0
    )
    vmem = pl.BlockSpec(memory_space=pltpu.VMEM)
    return pl.pallas_call(
        kernel,
        out_shape=tuple(outs),
        in_specs=[pl.BlockSpec(memory_space=pltpu.SMEM)] + [vmem] * n + [pl.BlockSpec(memory_space=pl.ANY)] * len(after),
        out_specs=tuple([vmem] * len(outs)),
        scratch_shapes=list(scratch),
        compiler_params=pltpu.CompilerParams(vmem_limit_bytes=limit * MIB),
        cost_estimate=cost,
        name=body.__qualname__.split(".")[0],
    )(ids, *args, *after)


def loop_tiles(size, tile, body):
    def step(j, carry):
        body(pl.ds(pl.multiple_of(j * tile, tile), tile))
        return carry

    lax.fori_loop(0, size // tile, step, 0)


def token_row(ids, core_rel, y_rel, rows):
    core = lax.rem(ids[2] + core_rel, 2)
    y = lax.rem(ids[1] + y_rel, NY)
    return pl.multiple_of((core * NY + y) * rows, rows)


def ordered_tokens(ids, rows, tokens):
    width = tokens.shape[1]

    def body(ids, t_ref, o_ref):
        for c in range(2):
            for y in range(NY):
                at = (c * NY + y) * rows
                o_ref[at:at + rows, :] = t_ref[pl.ds(token_row(ids, c, y, rows), rows), :]

    return call(body, ids, (tokens,), [shape((8 * rows, width))])[0]


def pre_products(ids, rows, ordered, weight):
    width, cols = weight.shape

    def body(ids, t_ref, w_ref, own_ref, other_ref):
        def step(at):
            acc = jnp.dot(t_ref[...], w_ref[:, at], preferred_element_type=F32).astype(BF)
            acc = acc.reshape(2, NY, rows, TILE)
            own_ref[:, :, at] = acc[0]
            other_ref[:, :, at] = acc[1]

        loop_tiles(cols, TILE, step)

    out = shape((NY, rows, cols))
    return call(
        body, ids, (ordered, weight), [out, out], flops=2 * 8 * rows * width * cols
    )


def split_pre(ids, owns, recvs):
    n = len(owns)
    _, rows, cols = owns[0].shape
    half = rows // 2

    def body(ids, *refs):
        a_refs, b_refs = refs[:n], refs[n:2 * n]
        o0, o1l, o1h, o2l, o2h, o3l, o3h = refs[2 * n:]

        def step(at):
            for i in range(n):
                o0[i, :, at] = a_refs[i][0, :, at].astype(F32) + b_refs[i][0, :, at].astype(F32)
                for y, l_ref, h_ref in ((1, o1l, o1h), (2, o2l, o2h), (3, o3l, o3h)):
                    total = a_refs[i][y, :, at].astype(F32) + b_refs[i][y, :, at].astype(F32)
                    l_ref[i, :, at] = total[:half].astype(BF)
                    h_ref[i, :, at] = total[half:].astype(BF)

        loop_tiles(cols, TILE, step)

    outs = [shape((n, rows, cols), F32)] + [shape((n, half, cols))] * 6
    return call(body, ids, (*owns, *recvs), outs)


def add_pair(a, b):
    return (a.astype(F32) + b.astype(F32)).astype(BF)


def ring_scatter(blocks):
    own, b1l, b1h, b2l, b2h, b3l, b3h = blocks
    relay_low = shift(b2l, "y", 1)
    relay_high = shift(b2h, "y", -1)
    direct_high = shift(b1h, "y", 1)
    direct_low = shift(b3l, "y", -1)
    both_low = shift(add_pair(b1l, relay_low), "y", 1)
    both_high = shift(add_pair(b3h, relay_high), "y", -1)
    return own, (both_low, direct_low), (both_high, direct_high)


def coefficients(ids, chunk, own, sums, after=()):
    n, rows, cols = own.shape
    half = rows // 2
    mine = slice(chunk * half, (chunk + 1) * half)
    inv_width = 1.0 / math.sqrt(D)

    def body(ids, own_ref, a, b, pay_ref, first_ref, second_ref):
        def step(at):
            gate, up, tangent = (
                own_ref[i, mine, at] + a[i, :, at].astype(F32) + b[i, :, at].astype(F32)
                for i in range(n)
            )
            tangent = tangent * inv_width
            sig = jax.nn.sigmoid(gate)
            first = sig * (1.0 + gate * (1.0 - sig)) * up
            second = sig * (1.0 - sig) * (2.0 + gate * (1.0 - 2.0 * sig)) * (tangent * up)
            pay_ref[0, :, at] = (gate * sig * up).astype(BF)
            pay_ref[1, :, at] = (first * tangent).astype(BF)
            first_ref[:, at] = first.astype(BF)
            second_ref[:, at] = second.astype(BF)

        loop_tiles(cols, TILE, step)

    outs = [shape((2, half, cols)), shape((half, cols)), shape((half, cols))]
    return call(body, ids, (own, *sums), outs, after=after)


def gather_y(value):
    return [value, shift(value, "y", -1), shift(value, "y", -2), shift(value, "y", -3)]


def swap_cores(values):
    return [shift(v, "core", 1) for v in values]


def ring_pair(near, far):
    near_low, near_high = shift(near, "y", 1), shift(near, "y", -1)
    far_low, far_high = shift(far, "y", 1), shift(far, "y", -1)
    across = [shift(near_low[0], "y", 1), shift(near_high[1], "y", -1)]
    beyond = [shift(v, "dp", 1) for v in across]
    return [near, far, near_high, far_high, near_low, far_low], across + beyond


def down_products(ids, pieces, down):
    _, rows, cols = pieces[0].shape
    width = down.shape[1]
    tile = width // NZ
    total = 8 * 2 * rows

    def body(ids, *refs):
        p_refs, d_ref, o_refs, lhs = refs[:8], refs[8], refs[9:13], refs[13]
        for i, p_ref in enumerate(p_refs):
            lhs[2 * rows * i:2 * rows * (i + 1), :] = p_ref[...].reshape(2 * rows, cols)

        def step(k, carry):
            at = pl.multiple_of(lax.rem(ids[3] + k, NZ) * tile, tile)
            acc = jnp.dot(
                lhs[...], d_ref[:, pl.ds(at, tile)], preferred_element_type=F32
            ).astype(BF)
            for i, o_ref in enumerate(o_refs):
                @pl.when(k == i)
                def _(o_ref=o_ref):
                    o_ref[...] = acc
            return carry

        lax.fori_loop(0, NZ, step, 0)

    outs = [shape((total, tile))] * NZ
    return call(
        body, ids, (*pieces, down), outs, [pltpu.VMEM((total, cols), BF)],
        flops=2 * total * width * cols, limit=12)


def spread(axis, blocks):
    first, *rest = blocks
    return [first] + [shift(v, axis, k + 1) for k, v in enumerate(rest)]


def sum_z(ids, parts):
    def body(ids, a, b, c, d, o_ref):
        total = a[...].astype(F32) + b[...].astype(F32) + c[...].astype(F32) + d[...].astype(F32)
        o_ref[...] = total.astype(BF)

    return call(body, ids, parts, [shape(parts[0].shape)])[0]


def residual(ids, chunk, rows, own, recv, target):
    total, cols = own.shape

    def body(ids, own_ref, recv_ref, t_ref, o_ref):
        column = pl.multiple_of(ids[3] * cols, cols)
        for c in range(2):
            for y in range(NY):
                at = (c * NY + y) * 2 * rows
                to = slice(at, at + 2 * rows)
                value = own_ref[to].astype(F32) + recv_ref[to].astype(F32)
                row = pl.multiple_of(token_row(ids, c, y, 2 * rows) + chunk * rows, rows)
                goal = t_ref[pl.ds(row, rows), pl.ds(column, cols)]
                o_ref[at:at + rows] = (value[:rows] - goal.astype(F32)).astype(BF)
                o_ref[at + rows:at + 2 * rows] = value[rows:].astype(BF)

    return call(body, ids, (own, recv, target), [shape((total, cols))])[0]


def back_products(ids, parts, down, rows, after=()):
    total, tile_k = parts[0].shape
    cols, width = down.shape

    def body(ids, *refs):
        f_refs, d_ref, own_ref, other_ref = refs[:NZ], refs[NZ], refs[NZ + 1], refs[NZ + 2]

        def step(at):
            acc = jnp.zeros((total, TILE), F32)
            for k, f_ref in enumerate(f_refs):
                to = pl.multiple_of(lax.rem(ids[3] + k, NZ) * tile_k, tile_k)
                acc += lax.dot_general(
                    f_ref[...], d_ref[at, pl.ds(to, tile_k)], (((1,), (1,)), ((), ())),
                    preferred_element_type=F32,
                )
            acc = acc.astype(BF).reshape(2, NY, 2, rows, TILE)
            own_ref[:, :, :, at] = acc[0]
            other_ref[:, :, :, at] = acc[1]

        loop_tiles(cols, TILE, step)

    out = shape((NY, 2, rows, cols))
    return call(
        body, ids, (*parts, down), [out, out], flops=2 * total * width * cols, limit=12, after=after)


def split_back(ids, own, recv):
    _, n, rows, cols = own.shape

    def body(ids, a_ref, b_ref, *outs):
        def step(at):
            for i in range(n):
                for y in range(NY):
                    total = a_ref[y, i, :, at].astype(F32) + b_ref[y, i, :, at].astype(F32)
                    outs[y][i, :, at] = total.astype(outs[y].dtype)

        loop_tiles(cols, TILE, step)

    outs = [shape((n, rows, cols), F32)] + [shape((n, rows, cols))] * 3
    return call(body, ids, (own, recv), outs)


def sum_at(refs, i, at):
    total = refs[0][i, :, at].astype(F32)
    for ref in refs[1:]:
        total += ref[i, :, at].astype(F32)
    return total


def errors(ids, chunk, terms, first, second, before=()):
    n, rows, cols = terms[0].shape

    def body(ids, *refs):
        (f_ref, s_ref), done, o_ref = refs[len(terms):len(terms) + 2], refs[len(terms) + 2:-1], refs[-1]
        mine = slice(chunk * rows, (chunk + 1) * rows)

        def step(at):
            back, back_dot = (sum_at(refs[:len(terms)], i, at) for i in range(2))
            f = f_ref[:, at].astype(F32)
            o_ref[0, mine, at] = (back * f).astype(BF)
            o_ref[1, mine, at] = (back * s_ref[:, at].astype(F32) + back_dot * f).astype(BF)
            for ref in done:
                o_ref[:, :chunk * rows, at] = ref[:, :, at]

        loop_tiles(cols, TILE, step)

    out = shape((n, (chunk + 1) * rows, cols))
    return call(body, ids, (*terms, first, second, *before), [out])[0]


def transposed_tokens(ids, tokens, other, rows):
    count, width = tokens.shape
    half = other.shape[1]

    def body(ids, t_ref, x_ref, o_ref, held):
        cols = pl.ds(pl.multiple_of(ids[0] * half, half), half)
        at = 0
        for c, y in [(c, y) for c in range(2) for y in (0, 1, 3)] + [(0, 2), (1, 2)]:
            row = pl.ds(token_row(ids, c, y, rows), rows)
            held[at:at + rows, :] = t_ref[row, cols]
            held[at + rows:at + 2 * rows, :] = x_ref[row, :]
            at += 2 * rows
        o_ref[...] = held[...].T

    return call(
        body, ids, (tokens, other), [shape((half, 2 * count))],
        [pltpu.VMEM((2 * count, half), BF)],
    )[0]


def outer_products(ids, lhs, pieces, halves, probe):
    out_rows, count = lhs.shape
    _, rows, cols = pieces[0].shape
    token_scale = 1.0 / math.sqrt(count)
    inv_width = 1.0 / math.sqrt(D)
    n, m = len(pieces), len(pieces) + len(halves)

    def body(ids, l_ref, *refs):
        p_refs, probe_ref, g_ref, h_ref = refs[:n], refs[m], refs[m + 1], refs[m + 2]
        probe_rows = pl.ds(pl.multiple_of(ids[0] * out_rows, out_rows), out_rows)

        def step(at):
            err = jnp.concatenate([p[0, :, at] for p in p_refs] + [p[:, at] for p in refs[n:m:2]], axis=0)
            g = jnp.dot(l_ref[...], err, preferred_element_type=F32) * token_scale
            g_ref[:, at] = g.astype(BF)
            err = jnp.concatenate([p[1, :, at] for p in p_refs] + [p[:, at] for p in refs[n + 1:m:2]], axis=0)
            hv = jnp.dot(l_ref[...], err, preferred_element_type=F32) * token_scale
            h_ref[:, at] = (probe_ref[probe_rows, at].astype(F32) * hv * inv_width).astype(BF)

        loop_tiles(cols, TILE, step)

    out = shape((out_rows, cols))
    return call(
        body, ids, (lhs, *pieces, *halves, probe), [out, out],
        flops=4 * out_rows * count * cols, limit=12,
    )


def on_device(tokens, target, gate_weight, up_weight, down_weight, probe_sign):
    ids = jnp.stack([lax.axis_index(a) for a in ("dp", "y", "core", "z", "xh")]).astype(jnp.int32)
    count, width = tokens.shape
    rows = count // 8
    half = width // 2
    other_cols = lax.dynamic_slice_in_dim(tokens, (1 - ids[0]) * half, half, 1)
    other_tokens = shift(other_cols, "dp", 1)
    lhs = transposed_tokens(ids, tokens, other_tokens, rows)
    ordered = ordered_tokens(ids, rows, tokens)
    pairs = [pre_products(ids, rows, ordered, w) for w in (gate_weight, up_weight, probe_sign)]
    recvs = swap_cores([other for _, other in pairs])
    whole, *sums = ring_scatter(split_pre(ids, [own for own, _ in pairs], recvs))
    done, before = (), ()
    for c in range(2):
        pay, first, second = coefficients(ids, c, whole, sums[c], before)
        before = (pay,)
        near = gather_y(pay)
        parts = spread("z", down_products(ids, near + swap_cores(near), down_weight))
        part = sum_z(ids, parts)
        err = residual(ids, c, rows // 2, part, shift(part, "xh", 1), target)
        parts = [err] + [shift(err, "z", -k) for k in range(1, NZ)]
        own, other = back_products(ids, parts, down_weight, rows // 2, () if c else (lhs,))
        terms = spread("y", split_back(ids, own, shift(other, "core", 1)))
        done = (errors(ids, c, terms, first, second, done),)
    near, across = ring_pair(done[0], shift(done[0], "dp", 1))
    return outer_products(
        ids, lhs, near + swap_cores(near), across + swap_cores(across), probe_sign
    )


def solution(mesh):
    fine = Mesh(mesh.devices.reshape(2, 4, 2, 4, 2), ("dp", "y", "core", "z", "xh"))
    width, hidden = ("y", "core"), ("z", "xh")
    return jax.shard_map(
        on_device,
        mesh=fine,
        in_specs=(
            P("dp", width),
            P("dp", width),
            P(width, hidden),
            P(width, hidden),
            P(hidden, width),
            P(width, hidden),
        ),
        out_specs=(P(("y", "core", "dp"), hidden), P(("y", "core", "dp"), hidden)),
        check_vma=False,
    )
```

```python
import functools
import math

import jax
import jax.numpy as jnp
from jax import lax
from jax.experimental import pallas as pl
from jax.experimental.pallas import tpu as pltpu
from jax.sharding import Mesh, PartitionSpec as P

D = 8192
TILE = 256
WIDE = 1792
BF = jnp.bfloat16
F32 = jnp.float32
NY = 4
NZ = 4
MIB = 1024 * 1024


def shift(value, axis, step):
    size = lax.axis_size(axis)
    return lax.ppermute(value, axis, [(i, (i + step) % size) for i in range(size)])


def shape(dims, dtype=BF):
    return jax.ShapeDtypeStruct(dims, dtype)


def nbytes(avals):
    return sum(math.prod(a.shape) * a.dtype.itemsize for a in avals)


def call(body, ids, args, outs, scratch=(), flops=0, limit=8, after=()):
    n = len(args)

    def kernel(ids, *refs):
        body(ids, *refs[:n], *refs[n + len(after):])

    cost = pl.CostEstimate(
        flops=flops, bytes_accessed=nbytes(args) + nbytes(outs), transcendentals=0
    )
    vmem = pl.BlockSpec(memory_space=pltpu.VMEM)
    return pl.pallas_call(
        kernel,
        out_shape=tuple(outs),
        in_specs=[pl.BlockSpec(memory_space=pltpu.SMEM)] + [vmem] * n + [pl.BlockSpec(memory_space=pl.ANY)] * len(after),
        out_specs=tuple([vmem] * len(outs)),
        scratch_shapes=list(scratch),
        compiler_params=pltpu.CompilerParams(vmem_limit_bytes=limit * MIB),
        cost_estimate=cost,
        name=body.__qualname__.split(".")[0],
    )(ids, *args, *after)


def loop_tiles(size, tile, body):
    def step(j, carry):
        body(pl.ds(pl.multiple_of(j * tile, tile), tile))
        return carry

    lax.fori_loop(0, size // tile, step, 0)


def token_row(ids, core_rel, y_rel, rows):
    core = lax.rem(ids[2] + core_rel, 2)
    y = lax.rem(ids[1] + y_rel, NY)
    return pl.multiple_of((core * NY + y) * rows, rows)


def ordered_tokens(ids, rows, tokens):
    width = tokens.shape[1]

    def body(ids, t_ref, o_ref):
        for c in range(2):
            for y in range(NY):
                at = (c * NY + y) * rows
                o_ref[at:at + rows, :] = t_ref[pl.ds(token_row(ids, c, y, rows), rows), :]

    return call(body, ids, (tokens,), [shape((8 * rows, width))])[0]


def pre_products(ids, rows, ordered, weight):
    width, cols = weight.shape

    def body(ids, t_ref, w_ref, own_ref, other_ref):
        def step(at):
            acc = jnp.dot(t_ref[...], w_ref[:, at], preferred_element_type=F32).astype(BF)
            acc = acc.reshape(2, NY, rows, WIDE)
            own_ref[:, :, at] = acc[0]
            other_ref[:, :, at] = acc[1]

        loop_tiles(cols, WIDE, step)

    out = shape((NY, rows, cols))
    return call(
        body, ids, (ordered, weight), [out, out], flops=2 * 8 * rows * width * cols
    )


def split_pre(ids, owns, recvs):
    n = len(owns)
    _, rows, cols = owns[0].shape
    half = rows // 2

    def body(ids, *refs):
        a_refs, b_refs = refs[:n], refs[n:2 * n]
        o0, o1l, o1h, o2l, o2h, o3l, o3h = refs[2 * n:]

        def step(at):
            for i in range(n):
                o0[i, :, at] = a_refs[i][0, :, at].astype(F32) + b_refs[i][0, :, at].astype(F32)
                for y, l_ref, h_ref in ((1, o1l, o1h), (2, o2l, o2h), (3, o3l, o3h)):
                    total = a_refs[i][y, :, at].astype(F32) + b_refs[i][y, :, at].astype(F32)
                    l_ref[i, :, at] = total[:half].astype(BF)
                    h_ref[i, :, at] = total[half:].astype(BF)

        loop_tiles(cols, TILE, step)

    outs = [shape((n, rows, cols), F32)] + [shape((n, half, cols))] * 6
    return call(body, ids, (*owns, *recvs), outs)


def add_pair(a, b):
    return (a.astype(F32) + b.astype(F32)).astype(BF)


def ring_scatter(blocks):
    own, b1l, b1h, b2l, b2h, b3l, b3h = blocks
    relay_low = shift(b2l, "y", 1)
    relay_high = shift(b2h, "y", -1)
    direct_high = shift(b1h, "y", 1)
    direct_low = shift(b3l, "y", -1)
    both_low = shift(add_pair(b1l, relay_low), "y", 1)
    both_high = shift(add_pair(b3h, relay_high), "y", -1)
    return own, (both_low, direct_low), (both_high, direct_high)


def coefficients(ids, chunk, own, sums, after=()):
    n, rows, cols = own.shape
    half = rows // 2
    mine = slice(chunk * half, (chunk + 1) * half)
    inv_width = 1.0 / math.sqrt(D)

    def body(ids, own_ref, a, b, pay_ref, first_ref, second_ref):
        def step(at):
            gate, up, tangent = (
                own_ref[i, mine, at] + a[i, :, at].astype(F32) + b[i, :, at].astype(F32)
                for i in range(n)
            )
            tangent = tangent * inv_width
            sig = jax.nn.sigmoid(gate)
            first = sig * (1.0 + gate * (1.0 - sig)) * up
            second = sig * (1.0 - sig) * (2.0 + gate * (1.0 - 2.0 * sig)) * (tangent * up)
            pay_ref[0, :, at] = (gate * sig * up).astype(BF)
            pay_ref[1, :, at] = (first * tangent).astype(BF)
            first_ref[:, at] = first.astype(BF)
            second_ref[:, at] = second.astype(BF)

        loop_tiles(cols, TILE, step)

    outs = [shape((2, half, cols)), shape((half, cols)), shape((half, cols))]
    return call(body, ids, (own, *sums), outs, after=after)


def gather_y(value):
    return [value, shift(value, "y", -1), shift(value, "y", -2), shift(value, "y", -3)]


def swap_cores(values):
    return [shift(v, "core", 1) for v in values]


def ring_pair(near, far):
    near_low, near_high = shift(near, "y", 1), shift(near, "y", -1)
    across = shift(near_high, "y", -1)
    far_low, far_high = shift(far, "y", 1), shift(far, "y", -1)
    return [near, far, near_high, far_high, near_low, far_low], [across, shift(across, "dp", 1)]


def down_products(ids, pieces, down):
    _, rows, cols = pieces[0].shape
    width = down.shape[1]
    tile = width // NZ
    total = 8 * 2 * rows

    def body(ids, *refs):
        p_refs, d_ref, o_refs, lhs = refs[:8], refs[8], refs[9:13], refs[13]
        for i, p_ref in enumerate(p_refs):
            lhs[2 * rows * i:2 * rows * (i + 1), :] = p_ref[...].reshape(2 * rows, cols)

        def step(k, carry):
            at = pl.multiple_of(lax.rem(ids[3] + k, NZ) * tile, tile)
            acc = jnp.dot(
                lhs[...], d_ref[:, pl.ds(at, tile)], preferred_element_type=F32
            ).astype(BF)
            for i, o_ref in enumerate(o_refs):
                @pl.when(k == i)
                def _(o_ref=o_ref):
                    o_ref[...] = acc
            return carry

        lax.fori_loop(0, NZ, step, 0)

    outs = [shape((total, tile))] * NZ
    return call(
        body, ids, (*pieces, down), outs, [pltpu.VMEM((total, cols), BF)],
        flops=2 * total * width * cols, limit=12)


def spread(axis, blocks):
    first, *rest = blocks
    return [first] + [shift(v, axis, k + 1) for k, v in enumerate(rest)]


def sum_z(ids, parts):
    def body(ids, a, b, c, d, o_ref):
        total = a[...].astype(F32) + b[...].astype(F32) + c[...].astype(F32) + d[...].astype(F32)
        o_ref[...] = total.astype(BF)

    return call(body, ids, parts, [shape(parts[0].shape)])[0]


def residual(ids, chunk, rows, own, recv, target):
    total, cols = own.shape

    def body(ids, own_ref, recv_ref, t_ref, o_ref):
        column = pl.multiple_of(ids[3] * cols, cols)
        for c in range(2):
            for y in range(NY):
                at = (c * NY + y) * 2 * rows
                to = slice(at, at + 2 * rows)
                value = own_ref[to].astype(F32) + recv_ref[to].astype(F32)
                row = pl.multiple_of(token_row(ids, c, y, 2 * rows) + chunk * rows, rows)
                goal = t_ref[pl.ds(row, rows), pl.ds(column, cols)]
                o_ref[at:at + rows] = (value[:rows] - goal.astype(F32)).astype(BF)
                o_ref[at + rows:at + 2 * rows] = value[rows:].astype(BF)

    return call(body, ids, (own, recv, target), [shape((total, cols))])[0]


def back_products(ids, parts, down, rows, after=()):
    total, tile_k = parts[0].shape
    cols, width = down.shape

    def body(ids, *refs):
        f_refs, d_ref, own_ref, other_ref = refs[:NZ], refs[NZ], refs[NZ + 1], refs[NZ + 2]

        def step(at):
            acc = jnp.zeros((total, WIDE), F32)
            for k, f_ref in enumerate(f_refs):
                to = pl.multiple_of(lax.rem(ids[3] + k, NZ) * tile_k, tile_k)
                acc += lax.dot_general(
                    f_ref[...], d_ref[at, pl.ds(to, tile_k)], (((1,), (1,)), ((), ())),
                    preferred_element_type=F32,
                )
            acc = acc.astype(BF).reshape(2, NY, 2, rows, WIDE)
            own_ref[:, :, :, at] = acc[0]
            other_ref[:, :, :, at] = acc[1]

        loop_tiles(cols, WIDE, step)

    out = shape((NY, 2, rows, cols))
    return call(
        body, ids, (*parts, down), [out, out], flops=2 * total * width * cols, limit=16, after=after)


def split_back(ids, own, recv):
    _, n, rows, cols = own.shape

    def body(ids, a_ref, b_ref, *outs):
        def step(at):
            for i in range(n):
                for y in range(NY):
                    total = a_ref[y, i, :, at].astype(F32) + b_ref[y, i, :, at].astype(F32)
                    outs[y][i, :, at] = total.astype(outs[y].dtype)

        loop_tiles(cols, TILE, step)

    outs = [shape((n, rows, cols), F32)] + [shape((n, rows, cols))] * 3
    return call(body, ids, (own, recv), outs)


def sum_at(refs, i, at):
    total = refs[0][i, :, at].astype(F32)
    for ref in refs[1:]:
        total += ref[i, :, at].astype(F32)
    return total


def errors(ids, chunk, terms, first, second, before=()):
    n, rows, cols = terms[0].shape

    def body(ids, *refs):
        (f_ref, s_ref), done, o_ref = refs[len(terms):len(terms) + 2], refs[len(terms) + 2:-1], refs[-1]
        mine = slice(chunk * rows, (chunk + 1) * rows)

        def step(at):
            back, back_dot = (sum_at(refs[:len(terms)], i, at) for i in range(2))
            f = f_ref[:, at].astype(F32)
            o_ref[0, mine, at] = (back * f).astype(BF)
            o_ref[1, mine, at] = (back * s_ref[:, at].astype(F32) + back_dot * f).astype(BF)
            for ref in done:
                o_ref[:, :chunk * rows, at] = ref[:, :, at]

        loop_tiles(cols, TILE, step)

    out = shape((n, (chunk + 1) * rows, cols))
    return call(body, ids, (*terms, first, second, *before), [out])[0]


def transposed_tokens(ids, tokens, other, rows):
    count, width = tokens.shape
    half = other.shape[1]

    def body(ids, t_ref, x_ref, o_ref, held):
        cols = pl.ds(pl.multiple_of(ids[0] * half, half), half)
        at = 0
        for c, y in [(c, y) for c in range(2) for y in (0, 1, 3)] + [(0, 2), (1, 2)]:
            row = pl.ds(token_row(ids, c, y, rows), rows)
            held[at:at + rows, :] = t_ref[row, cols]
            held[at + rows:at + 2 * rows, :] = x_ref[row, :]
            at += 2 * rows
        o_ref[...] = held[...].T

    return call(
        body, ids, (tokens, other), [shape((half, 2 * count))],
        [pltpu.VMEM((2 * count, half), BF)],
    )[0]


def outer_products(ids, lhs, pieces, halves, probe):
    out_rows, count = lhs.shape
    _, rows, cols = pieces[0].shape
    token_scale = 1.0 / math.sqrt(count)
    inv_width = 1.0 / math.sqrt(D)
    n, m = len(pieces), len(pieces) + len(halves)

    def body(ids, l_ref, *refs):
        p_refs, probe_ref, g_ref, h_ref = refs[:n], refs[m], refs[m + 1], refs[m + 2]
        probe_rows = pl.ds(pl.multiple_of(ids[0] * out_rows, out_rows), out_rows)

        def step(at):
            err = jnp.concatenate([p[0, :, at] for p in p_refs] + [p[0, :, at] for p in refs[n:m]], axis=0)
            g = jnp.dot(l_ref[...], err, preferred_element_type=F32) * token_scale
            g_ref[:, at] = g.astype(BF)
            err = jnp.concatenate([p[1, :, at] for p in p_refs] + [p[1, :, at] for p in refs[n:m]], axis=0)
            hv = jnp.dot(l_ref[...], err, preferred_element_type=F32) * token_scale
            h_ref[:, at] = (probe_ref[probe_rows, at].astype(F32) * hv * inv_width).astype(BF)

        loop_tiles(cols, WIDE, step)

    out = shape((out_rows, cols))
    return call(
        body, ids, (lhs, *pieces, *halves, probe), [out, out],
        flops=4 * out_rows * count * cols, limit=16,
    )


def on_device(tokens, target, gate_weight, up_weight, down_weight, probe_sign):
    ids = jnp.stack([lax.axis_index(a) for a in ("dp", "y", "core", "z", "xh")]).astype(jnp.int32)
    count, width = tokens.shape
    rows = count // 8
    half = width // 2
    other_cols = lax.dynamic_slice_in_dim(tokens, (1 - ids[0]) * half, half, 1)
    other_tokens = shift(other_cols, "dp", 1)
    lhs = transposed_tokens(ids, tokens, other_tokens, rows)
    ordered = ordered_tokens(ids, rows, tokens)
    pairs = [pre_products(ids, rows, ordered, w) for w in (gate_weight, up_weight, probe_sign)]
    recvs = swap_cores([other for _, other in pairs])
    whole, *sums = ring_scatter(split_pre(ids, [own for own, _ in pairs], recvs))
    done, before = (), ()
    for c in range(2):
        pay, first, second = coefficients(ids, c, whole, sums[c], before)
        before = (pay,)
        near = gather_y(pay)
        parts = spread("z", down_products(ids, near + swap_cores(near), down_weight))
        part = sum_z(ids, parts)
        err = residual(ids, c, rows // 2, part, shift(part, "xh", 1), target)
        parts = [err] + [shift(err, "z", -k) for k in range(1, NZ)]
        own, other = back_products(ids, parts, down_weight, rows // 2, () if c else (lhs,))
        terms = spread("y", split_back(ids, own, shift(other, "core", 1)))
        done = (errors(ids, c, terms, first, second, done),)
    near, across = ring_pair(done[0], shift(done[0], "dp", 1))
    return outer_products(
        ids, lhs, near + swap_cores(near), across + swap_cores(across), probe_sign
    )


def solution(mesh):
    fine = Mesh(mesh.devices.reshape(2, 4, 2, 4, 2), ("dp", "y", "core", "z", "xh"))
    width, hidden = ("y", "core"), ("z", "xh")
    return jax.shard_map(
        on_device,
        mesh=fine,
        in_specs=(
            P("dp", width),
            P("dp", width),
            P(width, hidden),
            P(width, hidden),
            P(hidden, width),
            P(width, hidden),
        ),
        out_specs=(P(("y", "core", "dp"), hidden), P(("y", "core", "dp"), hidden)),
        check_vma=False,
    )
```

```python
import functools
import math

import jax
import jax.numpy as jnp
from jax import lax
from jax.experimental import pallas as pl
from jax.experimental.pallas import tpu as pltpu
from jax.sharding import Mesh, PartitionSpec as P

D = 8192
TILE = 256
WIDE = 1792
BF = jnp.bfloat16
F32 = jnp.float32
NY = 4
NZ = 4
MIB = 1024 * 1024


def shift(value, axis, step):
    size = lax.axis_size(axis)
    return lax.ppermute(value, axis, [(i, (i + step) % size) for i in range(size)])


def shape(dims, dtype=BF):
    return jax.ShapeDtypeStruct(dims, dtype)


def nbytes(avals):
    return sum(math.prod(a.shape) * a.dtype.itemsize for a in avals)


def call(body, ids, args, outs, scratch=(), flops=0, limit=8, after=()):
    n = len(args)

    def kernel(ids, *refs):
        body(ids, *refs[:n], *refs[n + len(after):])

    cost = pl.CostEstimate(
        flops=flops, bytes_accessed=nbytes(args) + nbytes(outs), transcendentals=0
    )
    vmem = pl.BlockSpec(memory_space=pltpu.VMEM)
    return pl.pallas_call(
        kernel,
        out_shape=tuple(outs),
        in_specs=[pl.BlockSpec(memory_space=pltpu.SMEM)] + [vmem] * n + [pl.BlockSpec(memory_space=pl.ANY)] * len(after),
        out_specs=tuple([vmem] * len(outs)),
        scratch_shapes=list(scratch),
        compiler_params=pltpu.CompilerParams(vmem_limit_bytes=limit * MIB),
        cost_estimate=cost,
        name=body.__qualname__.split(".")[0],
    )(ids, *args, *after)


def loop_tiles(size, tile, body):
    def step(j, carry):
        body(pl.ds(pl.multiple_of(j * tile, tile), tile))
        return carry

    lax.fori_loop(0, size // tile, step, 0)


def token_row(ids, core_rel, y_rel, rows):
    core = lax.rem(ids[2] + core_rel, 2)
    y = lax.rem(ids[1] + y_rel, NY)
    return pl.multiple_of((core * NY + y) * rows, rows)


def ordered_tokens(ids, rows, tokens):
    width = tokens.shape[1]

    def body(ids, t_ref, o_ref):
        for c in range(2):
            for y in range(NY):
                at = (c * NY + y) * rows
                o_ref[at:at + rows, :] = t_ref[pl.ds(token_row(ids, c, y, rows), rows), :]

    return call(body, ids, (tokens,), [shape((8 * rows, width))])[0]


def pre_products(ids, rows, ordered, weight):
    width, cols = weight.shape

    def body(ids, t_ref, w_ref, own_ref, other_ref):
        def step(at):
            acc = jnp.dot(t_ref[...], w_ref[:, at], preferred_element_type=F32).astype(BF)
            acc = acc.reshape(2, NY, rows, WIDE)
            own_ref[:, :, at] = acc[0]
            other_ref[:, :, at] = acc[1]

        loop_tiles(cols, WIDE, step)

    out = shape((NY, rows, cols))
    return call(
        body, ids, (ordered, weight), [out, out], flops=2 * 8 * rows * width * cols
    )


def split_pre(ids, owns, recvs):
    n = len(owns)
    _, rows, cols = owns[0].shape
    half = rows // 2

    def body(ids, *refs):
        a_refs, b_refs = refs[:n], refs[n:2 * n]
        o0, o1l, o1h, o2l, o2h, o3l, o3h = refs[2 * n:]

        def step(at):
            for i in range(n):
                o0[i, :, at] = a_refs[i][0, :, at].astype(F32) + b_refs[i][0, :, at].astype(F32)
                for y, l_ref, h_ref in ((1, o1l, o1h), (2, o2l, o2h), (3, o3l, o3h)):
                    total = a_refs[i][y, :, at].astype(F32) + b_refs[i][y, :, at].astype(F32)
                    l_ref[i, :, at] = total[:half].astype(BF)
                    h_ref[i, :, at] = total[half:].astype(BF)

        loop_tiles(cols, TILE, step)

    outs = [shape((n, rows, cols), F32)] + [shape((n, half, cols))] * 6
    return call(body, ids, (*owns, *recvs), outs)


def add_pair(a, b):
    return (a.astype(F32) + b.astype(F32)).astype(BF)


def ring_scatter(blocks):
    own, b1l, b1h, b2l, b2h, b3l, b3h = blocks
    relay_low = shift(b2l, "y", 1)
    relay_high = shift(b2h, "y", -1)
    direct_high = shift(b1h, "y", 1)
    direct_low = shift(b3l, "y", -1)
    both_low = shift(add_pair(b1l, relay_low), "y", 1)
    both_high = shift(add_pair(b3h, relay_high), "y", -1)
    return own, (both_low, direct_low), (both_high, direct_high)


def coefficients(ids, chunk, own, sums, after=()):
    n, rows, cols = own.shape
    half = rows // 2
    mine = slice(chunk * half, (chunk + 1) * half)
    inv_width = 1.0 / math.sqrt(D)

    def body(ids, own_ref, a, b, pay_ref, first_ref, second_ref):
        def step(at):
            gate, up, tangent = (
                own_ref[i, mine, at] + a[i, :, at].astype(F32) + b[i, :, at].astype(F32)
                for i in range(n)
            )
            tangent = tangent * inv_width
            sig = jax.nn.sigmoid(gate)
            first = sig * (1.0 + gate * (1.0 - sig)) * up
            second = sig * (1.0 - sig) * (2.0 + gate * (1.0 - 2.0 * sig)) * (tangent * up)
            pay_ref[0, :, at] = (gate * sig * up).astype(BF)
            pay_ref[1, :, at] = (first * tangent).astype(BF)
            first_ref[:, at] = first.astype(BF)
            second_ref[:, at] = second.astype(BF)

        loop_tiles(cols, TILE, step)

    outs = [shape((2, half, cols)), shape((half, cols)), shape((half, cols))]
    return call(body, ids, (own, *sums), outs, after=after)


def gather_y(value):
    return [value, shift(value, "y", -1), shift(value, "y", -2), shift(value, "y", -3)]


def swap_cores(values):
    return [shift(v, "core", 1) for v in values]


def ring_pair(near, far):
    near_low, near_high = shift(near, "y", 1), shift(near, "y", -1)
    across = shift(near_high, "y", -1)
    far_low, far_high = shift(far, "y", 1), shift(far, "y", -1)
    return [near, far, near_high, far_high, near_low, far_low], [across, shift(across, "dp", 1)]


def down_products(ids, pieces, down):
    _, rows, cols = pieces[0].shape
    width = down.shape[1]
    tile = width // NZ
    total = 8 * 2 * rows

    def body(ids, *refs):
        p_refs, d_ref, o_refs, (lhs, held) = refs[:8], refs[8], refs[9:13], refs[13:]
        for i, p_ref in enumerate(p_refs):
            lhs[2 * rows * i:2 * rows * (i + 1), :] = p_ref[...].reshape(2 * rows, cols)

        held[...] = jnp.dot(lhs[...], d_ref[...], preferred_element_type=F32).astype(BF)
        for k, o_ref in enumerate(o_refs):
            at = pl.multiple_of(lax.rem(ids[3] + k, NZ) * tile, tile)
            o_ref[...] = held[:, pl.ds(at, tile)]

    outs = [shape((total, tile))] * NZ
    return call(
        body, ids, (*pieces, down), outs, [pltpu.VMEM((total, cols), BF), pltpu.VMEM((total, width), BF)],
        flops=2 * total * width * cols, limit=12)


def spread(axis, blocks):
    first, *rest = blocks
    return [first] + [shift(v, axis, k + 1) for k, v in enumerate(rest)]


def sum_z(ids, parts):
    def body(ids, a, b, c, d, o_ref):
        total = a[...].astype(F32) + b[...].astype(F32) + c[...].astype(F32) + d[...].astype(F32)
        o_ref[...] = total.astype(BF)

    return call(body, ids, parts, [shape(parts[0].shape)])[0]


def residual(ids, chunk, rows, own, recv, target):
    total, cols = own.shape

    def body(ids, own_ref, recv_ref, t_ref, o_ref):
        column = pl.multiple_of(ids[3] * cols, cols)
        for c in range(2):
            for y in range(NY):
                at = (c * NY + y) * 2 * rows
                to = slice(at, at + 2 * rows)
                value = own_ref[to].astype(F32) + recv_ref[to].astype(F32)
                row = pl.multiple_of(token_row(ids, c, y, 2 * rows) + chunk * rows, rows)
                goal = t_ref[pl.ds(row, rows), pl.ds(column, cols)]
                o_ref[at:at + rows] = (value[:rows] - goal.astype(F32)).astype(BF)
                o_ref[at + rows:at + 2 * rows] = value[rows:].astype(BF)

    return call(body, ids, (own, recv, target), [shape((total, cols))])[0]


def back_products(ids, parts, down, rows, after=()):
    total, tile_k = parts[0].shape
    cols, width = down.shape

    def body(ids, *refs):
        f_refs, d_ref, own_ref, other_ref = refs[:NZ], refs[NZ], refs[NZ + 1], refs[NZ + 2]

        def step(at):
            acc = jnp.zeros((total, WIDE), F32)
            for k, f_ref in enumerate(f_refs):
                to = pl.multiple_of(lax.rem(ids[3] + k, NZ) * tile_k, tile_k)
                acc += lax.dot_general(
                    f_ref[...], d_ref[at, pl.ds(to, tile_k)], (((1,), (1,)), ((), ())),
                    preferred_element_type=F32,
                )
            acc = acc.astype(BF).reshape(2, NY, 2, rows, WIDE)
            own_ref[:, :, :, at] = acc[0]
            other_ref[:, :, :, at] = acc[1]

        loop_tiles(cols, WIDE, step)

    out = shape((NY, 2, rows, cols))
    return call(
        body, ids, (*parts, down), [out, out], flops=2 * total * width * cols, limit=16, after=after)


def split_back(ids, own, recv):
    _, n, rows, cols = own.shape

    def body(ids, a_ref, b_ref, *outs):
        def step(at):
            for i in range(n):
                for y in range(NY):
                    total = a_ref[y, i, :, at].astype(F32) + b_ref[y, i, :, at].astype(F32)
                    outs[y][i, :, at] = total.astype(outs[y].dtype)

        loop_tiles(cols, TILE, step)

    outs = [shape((n, rows, cols), F32)] + [shape((n, rows, cols))] * 3
    return call(body, ids, (own, recv), outs)


def sum_at(refs, i, at):
    total = refs[0][i, :, at].astype(F32)
    for ref in refs[1:]:
        total += ref[i, :, at].astype(F32)
    return total


def errors(ids, chunk, terms, first, second, before=()):
    n, rows, cols = terms[0].shape

    def body(ids, *refs):
        (f_ref, s_ref), done, o_ref = refs[len(terms):len(terms) + 2], refs[len(terms) + 2:-1], refs[-1]
        mine = slice(chunk * rows, (chunk + 1) * rows)

        def step(at):
            back, back_dot = (sum_at(refs[:len(terms)], i, at) for i in range(2))
            f = f_ref[:, at].astype(F32)
            o_ref[0, mine, at] = (back * f).astype(BF)
            o_ref[1, mine, at] = (back * s_ref[:, at].astype(F32) + back_dot * f).astype(BF)
            for ref in done:
                o_ref[:, :chunk * rows, at] = ref[:, :, at]

        loop_tiles(cols, TILE, step)

    out = shape((n, (chunk + 1) * rows, cols))
    return call(body, ids, (*terms, first, second, *before), [out])[0]


def transposed_tokens(ids, tokens, other, rows):
    count, width = tokens.shape
    half = other.shape[1]

    def body(ids, t_ref, x_ref, o_ref, held):
        cols = pl.ds(pl.multiple_of(ids[0] * half, half), half)
        at = 0
        for c, y in [(c, y) for c in range(2) for y in (0, 1, 3)] + [(0, 2), (1, 2)]:
            row = pl.ds(token_row(ids, c, y, rows), rows)
            held[at:at + rows, :] = t_ref[row, cols]
            held[at + rows:at + 2 * rows, :] = x_ref[row, :]
            at += 2 * rows
        o_ref[...] = held[...].T

    return call(
        body, ids, (tokens, other), [shape((half, 2 * count))],
        [pltpu.VMEM((2 * count, half), BF)],
    )[0]


def outer_products(ids, lhs, pieces, halves, probe):
    out_rows, count = lhs.shape
    _, rows, cols = pieces[0].shape
    token_scale = 1.0 / math.sqrt(count)
    inv_width = 1.0 / math.sqrt(D)
    n, m = len(pieces), len(pieces) + len(halves)

    def body(ids, l_ref, *refs):
        p_refs, probe_ref, g_ref, h_ref = refs[:n], refs[m], refs[m + 1], refs[m + 2]
        probe_rows = pl.ds(pl.multiple_of(ids[0] * out_rows, out_rows), out_rows)

        def step(at):
            err = jnp.concatenate([p[0, :, at] for p in p_refs] + [p[0, :, at] for p in refs[n:m]], axis=0)
            g = jnp.dot(l_ref[...], err, preferred_element_type=F32) * token_scale
            g_ref[:, at] = g.astype(BF)
            err = jnp.concatenate([p[1, :, at] for p in p_refs] + [p[1, :, at] for p in refs[n:m]], axis=0)
            hv = jnp.dot(l_ref[...], err, preferred_element_type=F32) * token_scale
            h_ref[:, at] = (probe_ref[probe_rows, at].astype(F32) * hv * inv_width).astype(BF)

        loop_tiles(cols, WIDE, step)

    out = shape((out_rows, cols))
    return call(
        body, ids, (lhs, *pieces, *halves, probe), [out, out],
        flops=4 * out_rows * count * cols, limit=16,
    )


def on_device(tokens, target, gate_weight, up_weight, down_weight, probe_sign):
    ids = jnp.stack([lax.axis_index(a) for a in ("dp", "y", "core", "z", "xh")]).astype(jnp.int32)
    count, width = tokens.shape
    rows = count // 8
    half = width // 2
    other_cols = lax.dynamic_slice_in_dim(tokens, (1 - ids[0]) * half, half, 1)
    other_tokens = shift(other_cols, "dp", 1)
    lhs = transposed_tokens(ids, tokens, other_tokens, rows)
    ordered = ordered_tokens(ids, rows, tokens)
    pairs = [pre_products(ids, rows, ordered, w) for w in (gate_weight, up_weight, probe_sign)]
    recvs = swap_cores([other for _, other in pairs])
    whole, *sums = ring_scatter(split_pre(ids, [own for own, _ in pairs], recvs))
    done, before = (), ()
    for c in range(2):
        pay, first, second = coefficients(ids, c, whole, sums[c], before)
        before = (pay,)
        near = gather_y(pay)
        parts = spread("z", down_products(ids, near + swap_cores(near), down_weight))
        part = sum_z(ids, parts)
        err = residual(ids, c, rows // 2, part, shift(part, "xh", 1), target)
        parts = [err] + [shift(err, "z", -k) for k in range(1, NZ)]
        own, other = back_products(ids, parts, down_weight, rows // 2, () if c else (lhs,))
        terms = spread("y", split_back(ids, own, shift(other, "core", 1)))
        done = (errors(ids, c, terms, first, second, done),)
    near, across = ring_pair(done[0], shift(done[0], "dp", 1))
    return outer_products(
        ids, lhs, near + swap_cores(near), across + swap_cores(across), probe_sign
    )


def solution(mesh):
    fine = Mesh(mesh.devices.reshape(2, 4, 2, 4, 2), ("dp", "y", "core", "z", "xh"))
    width, hidden = ("y", "core"), ("z", "xh")
    return jax.shard_map(
        on_device,
        mesh=fine,
        in_specs=(
            P("dp", width),
            P("dp", width),
            P(width, hidden),
            P(width, hidden),
            P(hidden, width),
            P(width, hidden),
        ),
        out_specs=(P(("y", "core", "dp"), hidden), P(("y", "core", "dp"), hidden)),
        check_vma=False,
    )
```
